128 devices in a mesh: expert: 64 (over z, y, x_hi, core), dp: 2 (over x_lo).
Axes of the slice: x: 4 (x_hi: 2, x_lo: 2; x = x_hi * 2 + x_lo), y: 4, z: 4, core: 2. Of those that a mesh axis runs over, the one named last changes fastest.
Arguments:
- tokens: bfloat16 [8192, 4096], P(('expert', 'dp')), may hold values from -6 to 6
- expert_ids: int32 [8192, 8], P(('expert', 'dp')), may hold values from 0 to 127, all different within a row; in each aligned block of 64 rows (0 to 63, 64 to 127, ...) at most 8 rows name the same one
- gate_up: bfloat16 [128, 4096, 1536], P('expert', None, 'dp'), may hold values from -0.09375 to 0.09375
Outputs:
- factors: float32 [128, 768, 768], P('expert', 'dp')
The draws below stay inside these ranges and needn't reach their ends.
Inputs may be any that keep to these rules, and one draw needn't show every extreme that they name: `expert_ids`: each token names 8 distinct experts. Within each device's aligned block of 64 tokens no expert is named more than 8 times, a bound that some block reaches.
All inputs are finite; a program needn't handle non-finite values.
Results may differ from the reference program's by a relative error of at most 0.004.
Values may be sent and summed in bfloat16 or wider, within the bound.
A program may use at most 192 MiB of HBM per device.

```python
import math
import jax
import jax.numpy as jnp
import numpy as np
from jax import lax

D = 4096
FW = 768
EXPERTS = 128
TOP = 8
TOK_DEV = 64
CAP = 8
TOKENS = 8192
ROWS_MEAN = 512
N_EXPERT = 64
N_DP = 2


def levels(key, extent, split, least, largest):
    loudness, own = 1.0, jax.random.fold_in(key, 6)
    for axis_at, blocks in split:
        steps = jnp.exp(jax.random.uniform(jax.random.fold_in(own, axis_at), (blocks,), jnp.float32, least / len(split), largest / len(split)))
        loudness = loudness * jnp.repeat(steps, extent[axis_at] // blocks).reshape([-1 if axis == axis_at else 1 for axis in range(len(extent))])
    return loudness


def assign_block(key, own, number, rows, count, top, bound, slope):
    sequence = jax.random.permutation(key, count)
    heavy_load, ordinary = shares(count, rows * top, bound, slope, True), shares(count, rows * top, bound, slope, False)
    places = jnp.arange(count)

    def named(sizes, rotation):
        used = int((sizes > 0).sum())
        fixed = max(1, used // 4)
        passed = fixed + (places - fixed + rotation * (used - fixed)) % max(1, count - fixed)
        return jnp.zeros((count,), jnp.int32).at[sequence[jnp.where(places < fixed, places, passed)]].set(jnp.asarray(sizes, jnp.int32))

    sizes = jnp.where(number % 4 == 0, named(heavy_load, number // 4), named(ordinary, number - number // 4 - 1))
    mixed = jax.random.permutation(jax.random.fold_in(own, 3), count)
    donor, taker = mixed[0:count // 2 * 2:2], mixed[1:count // 2 * 2:2]
    slack = jnp.minimum(sizes[donor] - 1, bound - sizes[taker]) // 2
    slack = jnp.where((donor == sequence[0]) | (taker == sequence[0]) | (sizes[taker] == 0), 0, jnp.maximum(slack, 0))
    passed = jax.random.randint(jax.random.fold_in(own, 4), (count // 2,), 0, 1 << 20) % (slack + 1)
    sizes = sizes.at[donor].add(-passed).at[taker].add(passed)
    members = jnp.searchsorted(jnp.cumsum(sizes), jnp.arange(rows * top), side="right").astype(jnp.int32)
    table = members.reshape(top, rows).T
    table = table[jax.random.permutation(jax.random.fold_in(own, 1), rows)]
    rotation = jax.random.randint(jax.random.fold_in(own, 2), (rows, 1), 0, top)
    return jnp.take_along_axis(table, (jnp.arange(top)[None, :] + rotation) % top, axis=1)


def shares(number_of, total, reach, slope, full):
    weights = [(1 << 20) // math.isqrt(rank ** slope) + 1 for rank in range(1, number_of + 1)]
    largest = reach if full else min(reach, max(-(-total // number_of), total * weights[0] // sum(weights)))
    least = 1 if total - largest >= number_of - 1 else 0
    given, surplus = [largest] + [least] * (number_of - 1), total - largest - least * (number_of - 1)
    while surplus > 0:
        movable = [i for i in range(1, number_of) if given[i] < largest] or [i for i in range(1, number_of) if given[i] < reach]
        mass, remaining = sum([weights[i] for i in movable]), surplus
        for i in movable:
            extra = min(reach - given[i], max(1, remaining * weights[i] // mass), surplus)
            given[i] = given[i] + extra
            surplus = surplus - extra
    return np.array(given)


def gaussian(own_key, shape, scale, reach, shards=(), kind=jnp.bfloat16):
    drawn = scale * jax.random.normal(own_key, shape, jnp.float32)
    if shards:
        drawn = drawn * levels(own_key, shape, shards, -0.22, 0.18)
    return jnp.clip(drawn, -reach, reach).astype(kind)


def setup_inputs(seed: int = 0) -> dict:
    key_of = jax.random.split(jax.random.key(seed), 4)
    tokens = gaussian(key_of[0], (TOKENS, D), 1.0, 6.0, ((0, 128),))
    expert_ids_keys = jax.random.split(jax.random.fold_in(key_of[1], 1), TOKENS // TOK_DEV)
    expert_ids_turns = jax.random.permutation(jax.random.fold_in(key_of[1], 3), TOKENS // TOK_DEV)
    expert_ids = jax.vmap(lambda own, number: assign_block(jax.random.fold_in(key_of[1], 2), own, number, TOK_DEV, EXPERTS, TOP, CAP, 2))(expert_ids_keys, expert_ids_turns).reshape((TOKENS, TOP))
    gate_up = gaussian(key_of[2], (EXPERTS, D, 2 * FW), D ** -0.5, 0.09375, ((0, 64), (2, 2)))
    return {"tokens": tokens, "expert_ids": expert_ids, "gate_up": gate_up}


damping = 0.25

def reference(tokens, expert_ids, gate_up):
    flat_ids = expert_ids.reshape(-1).astype(jnp.int32)
    owner = jnp.repeat(jnp.arange(TOKENS, dtype=jnp.int32), TOP)
    order = jnp.argsort(flat_ids, stable=True).astype(jnp.int32)
    counts = jnp.sum((flat_ids[:, None] == jnp.arange(EXPERTS, dtype=jnp.int32)[None, :]).astype(jnp.int32), axis=0).astype(jnp.int32)
    starts = (jnp.cumsum(counts) - counts).astype(jnp.int32)
    most_rows = N_EXPERT * N_DP * CAP
    scale = 1.0 / ROWS_MEAN
    identity = jnp.eye(FW, dtype=jnp.float32)

    def one_expert(index):
        slots = jnp.arange(most_rows, dtype=jnp.int32)
        valid = slots < counts[index]
        where_at = jnp.clip(starts[index] + slots, 0, TOKENS * TOP - 1).astype(jnp.int32)
        rows = tokens[owner[order[where_at]]]
        rows = jnp.where(valid[:, None], rows, jnp.zeros_like(rows))
        weight = lax.dynamic_index_in_dim(gate_up, index, 0, keepdims=False).reshape(D, 2 * FW)
        both = jnp.dot(rows.astype(jnp.float32), weight.astype(jnp.float32), preferred_element_type=jnp.float32).reshape(most_rows, 2, FW)
        hidden = (jax.nn.silu(both[:, 0, :]) * both[:, 1, :]).astype(jnp.bfloat16)
        gram = jnp.dot(hidden.T.astype(jnp.float32), hidden.astype(jnp.float32), preferred_element_type=jnp.float32)
        moment = gram * scale + damping * damping * identity
        return jnp.linalg.cholesky(moment).T
    return lax.map(one_expert, jnp.arange(EXPERTS, dtype=jnp.int32))
```

```python
import jax
import jax.numpy as jnp
from jax import lax
from jax.sharding import Mesh, PartitionSpec as P
from jax.experimental import pallas as pl
from jax.experimental.pallas import tpu as pltpu

damping = 0.25
capacity = 8
rows_mean = 512

N=768; B=128; NB=N//B
HI=lax.Precision.HIGHEST
def dotT(a,b):
    return lax.dot_general(a,b,(((0,),(0,)),((),())),precision=HI,preferred_element_type=jnp.float32)
def dot(a,b):
    return lax.dot_general(a,b,(((1,),(0,)),((),())),precision=HI,preferred_element_type=jnp.float32)
def factor_block(get, put_u, put_l):
    sub=lax.broadcasted_iota(jnp.int32,(8,128),0); lane=lax.broadcasted_iota(jnp.int32,(8,128),1)
    A=[get(i) for i in range(16)]
    E=[jnp.where(lane==sub+8*i,1.0,0.0).astype(jnp.float32) for i in range(16)]
    D=[jnp.zeros((8,128),jnp.float32) for i in range(16)]
    for j in range(128):
        q,s=divmod(j,8)
        cols=[jnp.broadcast_to(A[i][:,j:j+1],(8,128)) for i in range(q,16)]
        piv=jnp.broadcast_to(cols[0][s:s+1,:],(8,128))
        inv=1.0/piv
        D[q]=jnp.where(sub==s,piv,D[q])
        ra=jnp.broadcast_to(A[q][s:s+1,:],(8,128))*inv
        re=jnp.broadcast_to(E[q][s:s+1,:],(8,128))*inv
        for i in range(q,16):
            c=cols[i-q]
            if i==q:
                if s==7: continue
                c=jnp.where(sub>s,c,0.0)
            A[i]=A[i]-c*ra
            E[i]=E[i]-c*re
    for i in range(16):
        rs=lax.rsqrt(D[i])
        put_u(i, jnp.where(lane>=sub+8*i,A[i]*rs,0.0)); put_l(i, E[i]*rs)
def chol_kernel(g_ref, r_ref, a_ref, l_ref):
    a_ref[...]=g_ref[...]
    r_ref[...]=jnp.zeros_like(r_ref)
    for k in range(NB):
        o=k*B
        def put_u(i,v): r_ref[o+8*i:o+8*i+8,o:o+B]=v
        def put_l(i,v): l_ref[8*i:8*i+8,:]=v
        factor_block(lambda i:a_ref[o+8*i:o+8*i+8,o:o+B],put_u,put_l)
        if k<NB-1:
            p=dot(l_ref[...],a_ref[o:o+B,o+B:])
            r_ref[o:o+B,o+B:]=p
            for m in range(k+1,NB):
                x=m*B
                a_ref[x:x+B,x:]-=dotT(r_ref[o:o+B,x:x+B],r_ref[o:o+B,x:])
def upper_factor(g):
    return pl.pallas_call(chol_kernel,out_shape=jax.ShapeDtypeStruct((N,N),jnp.float32),
       in_specs=[pl.BlockSpec(memory_space=pltpu.VMEM)],out_specs=pl.BlockSpec(memory_space=pltpu.VMEM),
       scratch_shapes=[pltpu.VMEM((N,N),jnp.float32),pltpu.VMEM((B,B),jnp.float32)],
       compiler_params=pltpu.CompilerParams(vmem_limit_bytes=40<<20),name="upper_factor")(g)


def place(ids, names, capacity):
    blocks, tokens, _ = ids.shape
    named = jnp.any(ids[:, :, :, None] == names[None, None, None, :], axis=2)
    before = (jnp.arange(tokens)[:, None] > jnp.arange(tokens)[None, :]).astype(jnp.bfloat16)
    rank = jnp.einsum("st,btd->bsd", before, named.astype(jnp.bfloat16), preferred_element_type=jnp.float32)
    rank = jnp.where(named, rank.astype(jnp.int32), capacity)
    rank = rank.transpose(2, 0, 1)
    slot = jnp.arange(capacity, dtype=jnp.int32)
    block = jnp.arange(blocks, dtype=jnp.int32)
    chosen = (rank[:, None, None, :, :] == slot[None, None, :, None, None]) & (
        block[None, :, None, None, None] == block[None, None, None, :, None]
    )
    return chosen.astype(jnp.bfloat16).reshape(names.shape[0] * blocks * capacity, blocks * tokens)


def on_device(tokens, expert_ids, gate_up):
    z, y, c = lax.axis_index("z"), lax.axis_index("y"), lax.axis_index("core")
    xh, xl = lax.axis_index("xh"), lax.axis_index("xl")
    ring = ("xh", "xl")
    plane = ("z", "y", "core")
    width = gate_up.shape[2]
    send = lax.dynamic_index_in_dim(gate_up, 1 - xl, 0, keepdims=False)
    keep = lax.dynamic_index_in_dim(gate_up, xl, 0, keepdims=False)
    other = lax.ppermute(send, "xl", [(0, 1), (1, 0)])
    near = lax.all_gather(tokens, ring, axis=0, tiled=True)
    ids = lax.all_gather(expert_ids, ring, axis=0, tiled=True)
    ids = ids.reshape(4, tokens.shape[0], expert_ids.shape[1])
    d = jnp.arange(32, dtype=jnp.int32)
    names = (d // 2) * 8 + xh * 4 + (d % 2) * 2 + xl
    placing = place(ids, names, capacity)
    outgoing = jnp.dot(placing, near, preferred_element_type=jnp.float32).astype(jnp.bfloat16)
    rows = lax.all_to_all(outgoing.reshape(32, 32, tokens.shape[1]), plane, 0, 0, tiled=True)
    rows = rows.reshape(1024, tokens.shape[1])
    mine = jnp.dot(rows, keep, preferred_element_type=jnp.float32)
    theirs = jnp.dot(rows, other, preferred_element_type=jnp.float32)
    gate = jnp.where(xl == 0, mine, theirs)
    up = jnp.where(xl == 0, theirs, mine)
    hidden = (jax.nn.silu(gate) * up).astype(jnp.bfloat16)
    gram = lax.dot_general(hidden, hidden, (((0,), (0,)), ((), ())), preferred_element_type=jnp.float32)
    moment = gram * (1.0 / rows_mean) + damping * damping * jnp.eye(width, dtype=jnp.float32)
    factor = upper_factor(moment)
    half = width // 2
    away = lax.dynamic_slice_in_dim(factor, (1 - xl) * half, half, 0)
    here = lax.dynamic_slice_in_dim(factor, xl * half, half, 0)
    got = lax.ppermute(away, "xl", [(0, 1), (1, 0)])
    return jnp.stack([jnp.where(xl == 0, here, got), jnp.where(xl == 0, got, here)])


def solution(mesh):
    split = Mesh(mesh.devices.reshape(4, 4, 2, 2, 2), ("z", "y", "xh", "core", "xl"))
    every = ("z", "y", "xh", "core", "xl")
    experts = ("z", "y", "xh", "core")
    return jax.shard_map(
        on_device,
        mesh=split,
        in_specs=(P(every, None), P(every, None), P(experts, None, "xl")),
        out_specs=P(experts, "xl", None),
        check_vma=False,
    )
```

```python
import jax
import jax.numpy as jnp
from jax import lax
from jax.sharding import Mesh, PartitionSpec as P
from jax.experimental import pallas as pl
from jax.experimental.pallas import tpu as pltpu

damping = 0.25
capacity = 8
rows_mean = 512
experts = 128
part = 128
in_kernel = 768
MESH = pl.DeviceIdType.MESH

N=768; B=128; NB=N//B
HI=lax.Precision.HIGHEST
def dotT(a,b):
    return lax.dot_general(a,b,(((0,),(0,)),((),())),precision=HI,preferred_element_type=jnp.float32)
def dot(a,b):
    return lax.dot_general(a,b,(((1,),(0,)),((),())),precision=HI,preferred_element_type=jnp.float32)
def rep(v,s):
    return jnp.broadcast_to(v[s:s+1,:],(8,128))
def factor_block(get, put_u, put_l):
    sub=lax.broadcasted_iota(jnp.int32,(8,128),0); lane=lax.broadcasted_iota(jnp.int32,(8,128),1)
    A=[get(i) for i in range(16)]
    E=[jnp.where(lane==sub+8*i,1.0,0.0).astype(jnp.float32) for i in range(16)]
    for q in range(16):
        C=[[jnp.broadcast_to(A[i][:,8*q+m:8*q+m+1],(8,128)) for m in range(8)] for i in range(q,16)]
        p={(j,m):rep(C[0][m],j) for j in range(8) for m in range(j,8)}
        t=[rep(A[q],j) for j in range(8)]
        e=[rep(E[q],j) for j in range(8)]
        pivot=jnp.zeros((8,128),jnp.float32)
        for j in range(8):
            inv=1.0/p[j,j]
            pivot=jnp.where(sub==j,p[j,j],pivot)
            f={m:p[j,m]*inv for m in range(j+1,8)}
            for k in range(j+1,8):
                for m in range(k,8):
                    p[k,m]=p[k,m]-p[j,k]*f[m]
            for m in range(j+1,8):
                t[m]=t[m]-f[m]*t[j]
                e[m]=e[m]-f[m]*e[j]
            ts=t[j]*inv; es=e[j]*inv
            for i in range(q+1,16):
                c=C[i-q]
                for m in range(j+1,8):
                    c[m]=c[m]-c[j]*f[m]
                A[i]=A[i]-c[j]*ts
                E[i]=E[i]-c[j]*es
        rs=lax.rsqrt(pivot)
        u=t[0]; l=e[0]
        for j in range(1,8):
            u=jnp.where(sub==j,t[j],u); l=jnp.where(sub==j,e[j],l)
        put_u(q, jnp.where(lane>=sub+8*q,u*rs,0.0)); put_l(q, l*rs)
def chol_kernel(g_ref, r_ref, a_ref, l_ref, d_ref, u_ref):
    a_ref[...]=g_ref[...]
    r_ref[...]=jnp.zeros_like(r_ref)
    def put_u(i,v): u_ref[8*i:8*i+8,:]=v
    def put_l(i,v): l_ref[8*i:8*i+8,:]=v
    def fac():
        factor_block(lambda i:d_ref[8*i:8*i+8,:],put_u,put_l)
    for k in range(NB):
        o=k*B
        d_ref[...]=a_ref[o:o+B,o:o+B]
        lax.fori_loop(0,1,lambda i,c:(fac(),c)[1],0)
        r_ref[o:o+B,o:o+B]=u_ref[...]
        if k<NB-1:
            p=dot(l_ref[...],a_ref[o:o+B,o+B:])
            r_ref[o:o+B,o+B:]=p
            for m in range(k+1,NB):
                x=m*B
                a_ref[x:x+B,x:]-=dotT(r_ref[o:o+B,x:x+B],r_ref[o:o+B,x:])
def upper_factor(g):
    return pl.pallas_call(chol_kernel,out_shape=jax.ShapeDtypeStruct((N,N),jnp.float32),
       in_specs=[pl.BlockSpec(memory_space=pltpu.VMEM)],out_specs=pl.BlockSpec(memory_space=pltpu.VMEM),
       scratch_shapes=[pltpu.VMEM((N,N),jnp.float32)]+[pltpu.VMEM((B,B),jnp.float32)]*3,
       compiler_params=pltpu.CompilerParams(vmem_limit_bytes=40<<20),name="upper_factor")(g)


def slots(ids):
    tokens = ids.shape[0]
    names = jnp.arange(experts, dtype=jnp.int32)
    named = jnp.any(ids[:, :, None] == names[None, None, :], axis=1)
    before = (jnp.arange(tokens)[:, None] > jnp.arange(tokens)[None, :]).astype(jnp.bfloat16)
    rank = jnp.dot(before, named.astype(jnp.bfloat16), preferred_element_type=jnp.float32)
    rank = jnp.where(named, rank.astype(jnp.int32), capacity).T
    rank = rank.reshape(16, 2, 2, 2, tokens).transpose(1, 3, 0, 2, 4).reshape(4, 32, tokens)
    slot = jnp.arange(capacity, dtype=jnp.int32)
    chosen = rank[:, :, None, :] == slot[None, None, :, None]
    return chosen.astype(jnp.bfloat16).reshape(4, 32 * capacity, tokens)


def exchange_kernel(tok, plc, w, rows, other, tok_all, plc_all, out, near_s, near_r, far_s, far_r, w_s, w_r, own):
    z, y, c = lax.axis_index("z"), lax.axis_index("y"), lax.axis_index("core")
    xh, xl = lax.axis_index("xh"), lax.axis_index("xl")
    me_x = xh * 2 + xl
    me_p = (z * 4 + y) * 2 + c

    def on_ring(r):
        p = (me_x + r) % 4
        return p, (z, y, p // 2, c, p % 2)

    def on_plane(k):
        p = (me_p + k) % 32
        return p, (p // 8, (p // 2) % 4, xh, p % 2, xl)

    barrier = pltpu.get_barrier_semaphore()
    for r in range(1, 4):
        pl.semaphore_signal(barrier, 1, device_id=on_ring(r)[1], device_id_type=MESH)

    def greet(k, carry):
        pl.semaphore_signal(barrier, 1, device_id=on_plane(k)[1], device_id_type=MESH)
        return carry

    lax.fori_loop(1, 32, greet, 0)
    pl.semaphore_wait(barrier, 34)

    near = []
    for r in range(1, 4):
        p, device = on_ring(r)
        near.append(
            pltpu.make_async_remote_copy(
                tok, tok_all.at[me_x], near_s.at[2 * r - 2], near_r.at[2 * r - 2], device_id=device, device_id_type=MESH
            )
        )
        near.append(
            pltpu.make_async_remote_copy(
                plc.at[p], plc_all.at[me_x], near_s.at[2 * r - 1], near_r.at[2 * r - 1], device_id=device, device_id_type=MESH
            )
        )
    for copy in near:
        copy.start()
    here = [
        pltpu.make_async_copy(tok, tok_all.at[me_x], own.at[0]),
        pltpu.make_async_copy(plc.at[me_x], plc_all.at[me_x], own.at[1]),
    ]
    for copy in here:
        copy.start()
    for copy in here:
        copy.wait()
    for copy in near:
        copy.wait()
    weights = [
        pltpu.make_async_remote_copy(
            w.at[1 - xl, :, pl.ds(i * part, part)],
            other.at[:, pl.ds(i * part, part)],
            w_s.at[i],
            w_r.at[i],
            device_id=(z, y, xh, c, 1 - xl),
            device_id_type=MESH,
        )
        for i in range(other.shape[1] // part)
    ]
    for copy in weights:
        copy.start()

    def select(i, carry):
        columns = pl.ds(pl.multiple_of(i * 512, 512), 512)
        picked = [
            jnp.dot(plc_all[b], tok_all[b, :, columns], preferred_element_type=jnp.float32).reshape(32, 8, 512)
            for b in range(4)
        ]
        out[:, columns] = jnp.stack(picked, axis=1).reshape(1024, 512).astype(jnp.bfloat16)
        return carry

    lax.fori_loop(0, 8, select, 0)

    def far(k):
        p, device = on_plane(k)
        return pltpu.make_async_remote_copy(
            out.at[pl.ds(pl.multiple_of(p * 32, 32), 32), :],
            rows.at[pl.ds(pl.multiple_of(me_p * 32, 32), 32), :],
            far_s.at[k],
            far_r.at[k],
            device_id=device,
            device_id_type=MESH,
        )

    def start(k, carry):
        far(k).start()
        return carry

    def finish(k, carry):
        far(k).wait()
        return carry

    lax.fori_loop(1, 32, start, 0)
    mine = pl.ds(pl.multiple_of(me_p * 32, 32), 32)
    kept = pltpu.make_async_copy(out.at[mine, :], rows.at[mine, :], own.at[0])
    kept.start()
    lax.fori_loop(1, 32, finish, 0)
    kept.wait()
    for copy in weights:
        copy.wait()


def exchange(tokens, placing, gate_up):
    depth = tokens.shape[1]
    anywhere = pl.BlockSpec(memory_space=pl.ANY)
    dma = pltpu.SemaphoreType.DMA
    return pl.pallas_call(
        exchange_kernel,
        out_shape=(
            jax.ShapeDtypeStruct((1024, depth), jnp.bfloat16),
            jax.ShapeDtypeStruct((depth, in_kernel), jnp.bfloat16),
        ),
        in_specs=[anywhere] * 3,
        out_specs=(anywhere, anywhere),
        scratch_shapes=[
            pltpu.VMEM((4, 64, depth), jnp.bfloat16),
            pltpu.VMEM((4, 256, 64), jnp.bfloat16),
            pltpu.VMEM((1024, depth), jnp.bfloat16),
            dma((6,)),
            dma((6,)),
            dma((32,)),
            dma((32,)),
            dma((6,)),
            dma((6,)),
            dma((2,)),
        ],
        compiler_params=pltpu.CompilerParams(collective_id=1, has_side_effects=True, vmem_limit_bytes=48 << 20),
        name="exchange",
    )(tokens, placing, gate_up)


def on_device(tokens, expert_ids, gate_up):
    xl = lax.axis_index("xl")
    width = gate_up.shape[2]
    placing = slots(expert_ids)
    rows, other = exchange(tokens, placing, gate_up)
    keep = lax.dynamic_index_in_dim(gate_up, xl, 0, keepdims=False)
    mine = jnp.dot(rows, keep, preferred_element_type=jnp.float32)
    theirs = jnp.dot(rows, other, preferred_element_type=jnp.float32)
    gate = jnp.where(xl == 0, mine, theirs)
    up = jnp.where(xl == 0, theirs, mine)
    hidden = (jax.nn.silu(gate) * up).astype(jnp.bfloat16)
    gram = lax.dot_general(hidden, hidden, (((0,), (0,)), ((), ())), preferred_element_type=jnp.float32)
    moment = gram * (1.0 / rows_mean) + damping * damping * jnp.eye(width, dtype=jnp.float32)
    factor = upper_factor(moment)
    half = width // 2
    away = lax.dynamic_slice_in_dim(factor, (1 - xl) * half, half, 0)
    here = lax.dynamic_slice_in_dim(factor, xl * half, half, 0)
    got = lax.ppermute(away, "xl", [(0, 1), (1, 0)])
    return jnp.stack([jnp.where(xl == 0, here, got), jnp.where(xl == 0, got, here)])


def solution(mesh):
    split = Mesh(mesh.devices.reshape(4, 4, 2, 2, 2), ("z", "y", "xh", "core", "xl"))
    every = ("z", "y", "xh", "core", "xl")
    holders = ("z", "y", "xh", "core")
    return jax.shard_map(
        on_device,
        mesh=split,
        in_specs=(P(every, None), P(every, None), P(holders, None, "xl")),
        out_specs=P(holders, "xl", None),
        check_vma=False,
    )
```

```python
import jax
import jax.numpy as jnp
from jax import lax
from jax.sharding import Mesh, PartitionSpec as P
from jax.experimental import pallas as pl
from jax.experimental.pallas import tpu as pltpu

damping = 0.25
capacity = 8
rows_mean = 512
experts = 128
parts = ((0, 256), (256, 256), (512, 128), (640, 128))
MESH = pl.DeviceIdType.MESH

N=768; B=128; NB=N//B
HI=lax.Precision.HIGHEST
def dotT(a,b):
    return lax.dot_general(a,b,(((0,),(0,)),((),())),precision=HI,preferred_element_type=jnp.float32)
def dot(a,b):
    return lax.dot_general(a,b,(((1,),(0,)),((),())),precision=HI,preferred_element_type=jnp.float32)
def rep(v,s):
    return jnp.broadcast_to(v[s:s+1,:],(8,128))
def factor_block(get, put_u, put_l):
    sub=lax.broadcasted_iota(jnp.int32,(8,128),0); lane=lax.broadcasted_iota(jnp.int32,(8,128),1)
    A=[get(i) for i in range(16)]
    E=[jnp.where(lane==sub+8*i,1.0,0.0).astype(jnp.float32) for i in range(16)]
    for q in range(16):
        C=[[jnp.broadcast_to(A[i][:,8*q+m:8*q+m+1],(8,128)) for m in range(8)] for i in range(q,16)]
        p={(j,m):rep(C[0][m],j) for j in range(8) for m in range(j,8)}
        t=[rep(A[q],j) for j in range(8)]
        e=[rep(E[q],j) for j in range(8)]
        pivot=jnp.zeros((8,128),jnp.float32)
        for j in range(8):
            inv=1.0/p[j,j]
            pivot=jnp.where(sub==j,p[j,j],pivot)
            f={m:p[j,m]*inv for m in range(j+1,8)}
            for k in range(j+1,8):
                for m in range(k,8):
                    p[k,m]=p[k,m]-p[j,k]*f[m]
            for m in range(j+1,8):
                t[m]=t[m]-f[m]*t[j]
                e[m]=e[m]-f[m]*e[j]
            ts=t[j]*inv; es=e[j]*inv
            for i in range(q+1,16):
                c=C[i-q]
                for m in range(j+1,8):
                    c[m]=c[m]-c[j]*f[m]
                A[i]=A[i]-c[j]*ts
                E[i]=E[i]-c[j]*es
        rs=lax.rsqrt(pivot)
        u=t[0]; l=e[0]
        for j in range(1,8):
            u=jnp.where(sub==j,t[j],u); l=jnp.where(sub==j,e[j],l)
        put_u(q, jnp.where(lane>=sub+8*q,u*rs,0.0)); put_l(q, l*rs)


def slots(ids):
    tokens = ids.shape[0]
    names = jnp.arange(experts, dtype=jnp.int32)
    named = jnp.any(ids[:, :, None] == names[None, None, :], axis=1)
    before = (jnp.arange(tokens)[:, None] > jnp.arange(tokens)[None, :]).astype(jnp.bfloat16)
    rank = jnp.dot(before, named.astype(jnp.bfloat16), preferred_element_type=jnp.float32)
    rank = jnp.where(named, rank.astype(jnp.int32), capacity).T
    rank = rank.reshape(16, 2, 2, 2, tokens).transpose(1, 3, 0, 2, 4).reshape(4, 32, tokens)
    slot = jnp.arange(capacity, dtype=jnp.int32)
    chosen = rank[:, :, None, :] == slot[None, None, :, None]
    return chosen.astype(jnp.bfloat16).reshape(4, 32 * capacity, tokens)


def silu(v):
    return v / (1.0 + jnp.exp(-v))


def expert_kernel(
    tok, plc, w, out,
    tok_all, plc_all, outgoing, rows, keep, other, local, hidden, hidden_t, column, upper, lower, inverse, block, block_u,
    give, take, final,
    near_s, near_r, far_s, far_r, w_s, w_r, r_s, r_r, own,
):
    z, y, c = lax.axis_index("z"), lax.axis_index("y"), lax.axis_index("core")
    xh, xl = lax.axis_index("xh"), lax.axis_index("xl")
    me_x = xh * 2 + xl
    me_p = (z * 4 + y) * 2 + c
    partner = (z, y, xh, c, 1 - xl)

    def on_ring(r):
        p = (me_x + r) % 4
        return p, (z, y, p // 2, c, p % 2)

    def on_plane(k):
        p = (me_p + k) % 32
        return p, (p // 8, (p // 2) % 4, xh, p % 2, xl)

    def remote(src, dst, send, recv, device):
        return pltpu.make_async_remote_copy(src, dst, send, recv, device_id=device, device_id_type=MESH)

    keeping = pltpu.make_async_copy(w.at[xl], keep, own.at[0])
    keeping.start()
    here = [
        pltpu.make_async_copy(tok, tok_all.at[me_x], own.at[1]),
        pltpu.make_async_copy(plc.at[me_x], plc_all.at[me_x], own.at[2]),
    ]
    for copy in here:
        copy.start()

    barrier = pltpu.get_barrier_semaphore()
    for r in range(1, 4):
        pl.semaphore_signal(barrier, 1, device_id=on_ring(r)[1], device_id_type=MESH)

    def greet(k, carry):
        pl.semaphore_signal(barrier, 1, device_id=on_plane(k)[1], device_id_type=MESH)
        return carry

    lax.fori_loop(1, 32, greet, 0)
    pl.semaphore_wait(barrier, 34)

    right, to_right = on_ring(1)
    opposite, to_opposite = on_ring(2)
    left, to_left = on_ring(3)
    first, second = pl.ds(0, 32), pl.ds(32, 32)
    tok_right = remote(tok, tok_all.at[me_x], near_s.at[0], near_r.at[0], to_right)
    tok_left = remote(tok, tok_all.at[me_x], near_s.at[1], near_r.at[1], to_left)
    on_right = remote(tok_all.at[left, first], tok_all.at[left, first], near_s.at[2], near_r.at[2], to_right)
    on_left = remote(tok_all.at[right, second], tok_all.at[right, second], near_s.at[3], near_r.at[3], to_left)
    named = [
        remote(plc.at[p], plc_all.at[me_x], near_s.at[i], near_r.at[i], device)
        for i, p, device in ((4, right, to_right), (5, opposite, to_opposite), (6, left, to_left))
    ]
    tok_right.start()
    tok_left.start()
    for copy in named:
        copy.start()
    upper[...] = jnp.zeros_like(upper)
    final[...] = jnp.zeros_like(final)
    tok_right.wait_recv()
    on_right.start()
    tok_left.wait_recv()
    on_left.start()
    for copy in here + named:
        copy.wait()
    tok_right.wait_send()
    tok_left.wait_send()
    on_right.wait()
    on_left.wait()

    weights = []
    for i, (at, size) in enumerate(parts):
        columns = pl.ds(at, size)
        weights.append(remote(w.at[1 - xl, :, columns], other.at[:, columns], w_s.at[i], w_r.at[i], partner))
        weights[i].start()

    def select(i, carry):
        columns = pl.ds(pl.multiple_of(i * 512, 512), 512)
        picked = [
            jnp.dot(plc_all[b], tok_all[b, :, columns], preferred_element_type=jnp.float32).reshape(32, 8, 512)
            for b in range(4)
        ]
        outgoing[:, columns] = jnp.stack(picked, axis=1).reshape(1024, 512).astype(jnp.bfloat16)
        return carry

    lax.fori_loop(0, 8, select, 0)

    def far(k):
        p, device = on_plane(k)
        return remote(
            outgoing.at[pl.ds(pl.multiple_of(p * 32, 32), 32), :],
            rows.at[pl.ds(pl.multiple_of(k * 32, 32), 32), :],
            far_s.at[k],
            far_r.at[k],
            device,
        )

    def start(k, carry):
        far(k).start()
        return carry

    def arrive(k, carry):
        far(k).wait()
        return carry

    lax.fori_loop(1, 32, start, 0)
    kept = pltpu.make_async_copy(
        outgoing.at[pl.ds(pl.multiple_of(me_p * 32, 32), 32), :], rows.at[pl.ds(0, 32), :], own.at[1]
    )
    kept.start()
    kept.wait()
    keeping.wait()

    for g in range(4):
        lax.fori_loop(max(1, 8 * g), 8 * g + 8, arrive, 0)
        at = pl.ds(256 * g, 256)
        local[at, :] = jnp.dot(rows[at, :], keep[...], preferred_element_type=jnp.float32)

    def project(at, size):
        def tile(i, carry):
            some = pl.ds(pl.multiple_of(i * 512, 512), 512)
            theirs = jnp.dot(rows[some, :], other[:, at : at + size], preferred_element_type=jnp.float32)
            mine = local[some, at : at + size]
            gate = jnp.where(xl == 0, mine, theirs)
            up = jnp.where(xl == 0, theirs, mine)
            h = silu(gate) * up
            hidden[some, at : at + size] = h.astype(jnp.bfloat16)
            hidden_t[at : at + size, some] = h.T.astype(jnp.bfloat16)
            return carry

        lax.fori_loop(0, 2, tile, 0)

    eye = (lax.broadcasted_iota(jnp.int32, (B, B), 0) == lax.broadcasted_iota(jnp.int32, (B, B), 1)).astype(jnp.float32)

    def put_u(i, v):
        block_u[8 * i : 8 * i + 8, :] = v

    def factor_column(k):
        o, n = B * k, B * (k + 1)
        column[0:n, :] = jnp.dot(hidden_t[0:n, :], hidden[:, o:n], preferred_element_type=jnp.float32) * (1.0 / rows_mean)
        for i in range(k):
            a, b = B * i, B * (i + 1)
            solved = dot(inverse[i], column[a:b, :])
            upper[a:b, o:n] = solved
            if i + 1 < k:
                column[b:o, :] -= dot(lower[b:o, a:b], solved)
        pivot = column[o:n, :] + damping * damping * eye
        if k:
            turned = upper[0:o, o:n].T
            lower[o:n, 0:o] = turned
            pivot = pivot - dot(turned, upper[0:o, o:n])
        block[...] = pivot

        def put_l(i, v):
            inverse[k, 8 * i : 8 * i + 8, :] = v

        def once(i, carry):
            factor_block(lambda i: block[8 * i : 8 * i + 8, :], put_u, put_l)
            return carry

        lax.fori_loop(0, 1, once, 0)
        upper[o:n, o:n] = block_u[...]

    half = final.shape[0]
    pieces = []
    for k in range(NB):
        for i, (at, size) in enumerate(parts):
            if at == B * k:
                weights[i].wait_recv()
                project(at, size)
        factor_column(k)
        n = min(half, B * (k + 1))
        give[k, 0:n, :] = upper[pl.ds(pl.multiple_of((1 - xl) * half, half), n), B * k : B * k + B].astype(jnp.bfloat16)
        pieces.append(remote(give.at[k, pl.ds(0, n)], take.at[k, pl.ds(0, n)], r_s.at[k], r_r.at[k], partner))
        pieces[k].start()
    mine = pltpu.make_async_copy(upper.at[pl.ds(pl.multiple_of(xl * half, half), half), :], out.at[xl], own.at[0])
    mine.start()
    for k in range(NB):
        n = min(half, B * (k + 1))
        pieces[k].wait()
        final[0:n, B * k : B * k + B] = take[k, 0:n, :].astype(jnp.float32)
    theirs = pltpu.make_async_copy(final, out.at[1 - xl], own.at[1])
    theirs.start()
    for copy in weights:
        copy.wait_send()
    mine.wait()
    theirs.wait()


def on_device(tokens, expert_ids, gate_up):
    depth = tokens.shape[1]
    width = gate_up.shape[2]
    half = width // 2
    placing = slots(expert_ids)
    anywhere = pl.BlockSpec(memory_space=pl.ANY)
    dma = pltpu.SemaphoreType.DMA
    bf16, f32 = jnp.bfloat16, jnp.float32
    return pl.pallas_call(
        expert_kernel,
        out_shape=jax.ShapeDtypeStruct((2, half, width), f32),
        in_specs=[anywhere] * 3,
        out_specs=anywhere,
        scratch_shapes=[
            pltpu.VMEM((4, 64, depth), bf16),
            pltpu.VMEM((4, 256, 64), bf16),
            pltpu.VMEM((1024, depth), bf16),
            pltpu.VMEM((1024, depth), bf16),
            pltpu.VMEM((depth, width), bf16),
            pltpu.VMEM((depth, width), bf16),
            pltpu.VMEM((1024, width), f32),
            pltpu.VMEM((1024, width), bf16),
            pltpu.VMEM((width, 1024), bf16),
            pltpu.VMEM((width, B), f32),
            pltpu.VMEM((width, width), f32),
            pltpu.VMEM((width, width), f32),
            pltpu.VMEM((NB, B, B), f32),
            pltpu.VMEM((B, B), f32),
            pltpu.VMEM((B, B), f32),
            pltpu.VMEM((NB, half, B), bf16),
            pltpu.VMEM((NB, half, B), bf16),
            pltpu.VMEM((half, width), f32),
            dma((7,)),
            dma((7,)),
            dma((32,)),
            dma((32,)),
            dma((len(parts),)),
            dma((len(parts),)),
            dma((NB,)),
            dma((NB,)),
            dma((3,)),
        ],
        compiler_params=pltpu.CompilerParams(collective_id=1, has_side_effects=True, vmem_limit_bytes=60 << 20),
        name="expert_factor",
    )(tokens, placing, gate_up)


def solution(mesh):
    split = Mesh(mesh.devices.reshape(4, 4, 2, 2, 2), ("z", "y", "xh", "core", "xl"))
    every = ("z", "y", "xh", "core", "xl")
    holders = ("z", "y", "xh", "core")
    return jax.shard_map(
        on_device,
        mesh=split,
        in_specs=(P(every, None), P(every, None), P(holders, None, "xl")),
        out_specs=P(holders, "xl", None),
        check_vma=False,
    )
```

```python
import jax
import jax.numpy as jnp
from jax import lax
from jax.sharding import Mesh, PartitionSpec as P
from jax.experimental import pallas as pl
from jax.experimental.pallas import tpu as pltpu

damping = 0.25
capacity = 8
rows_mean = 512
experts = 128
parts = ((0, 256), (256, 256), (512, 128), (640, 128))
MESH = pl.DeviceIdType.MESH

N=768; B=128; NB=N//B
HI=lax.Precision.HIGHEST
def dotT(a,b):
    return lax.dot_general(a,b,(((0,),(0,)),((),())),precision=HI,preferred_element_type=jnp.float32)
def dot(a,b):
    return lax.dot_general(a,b,(((1,),(0,)),((),())),precision=HI,preferred_element_type=jnp.float32)
def rep(v,s):
    return jnp.broadcast_to(v[s:s+1,:],(8,128))
def factor_block(get, put_u, put_l):
    sub=lax.broadcasted_iota(jnp.int32,(8,128),0); lane=lax.broadcasted_iota(jnp.int32,(8,128),1)
    A=[get(i) for i in range(16)]
    E=[jnp.where(lane==sub+8*i,1.0,0.0).astype(jnp.float32) for i in range(16)]
    for q in range(16):
        C=[[jnp.broadcast_to(A[i][:,8*q+m:8*q+m+1],(8,128)) for m in range(8)] for i in range(q,16)]
        p={(j,m):rep(C[0][m],j) for j in range(8) for m in range(j,8)}
        t=[rep(A[q],j) for j in range(8)]
        e=[rep(E[q],j) for j in range(8)]
        pivot=jnp.zeros((8,128),jnp.float32)
        for j in range(8):
            inv=1.0/p[j,j]
            pivot=jnp.where(sub==j,p[j,j],pivot)
            f={m:p[j,m]*inv for m in range(j+1,8)}
            for k in range(j+1,8):
                for m in range(k,8):
                    p[k,m]=p[k,m]-p[j,k]*f[m]
            for m in range(j+1,8):
                t[m]=t[m]-f[m]*t[j]
                e[m]=e[m]-f[m]*e[j]
            ts=t[j]*inv; es=e[j]*inv
            for i in range(q+1,16):
                c=C[i-q]
                for m in range(j+1,8):
                    c[m]=c[m]-c[j]*f[m]
                A[i]=A[i]-c[j]*ts
                E[i]=E[i]-c[j]*es
        rs=lax.rsqrt(pivot)
        u=t[0]; l=e[0]
        for j in range(1,8):
            u=jnp.where(sub==j,t[j],u); l=jnp.where(sub==j,e[j],l)
        put_u(q, jnp.where(lane>=sub+8*q,u*rs,0.0)); put_l(q, l*rs)


def slots(ids):
    tokens = ids.shape[0]
    names = jnp.arange(experts, dtype=jnp.int32)
    named = jnp.any(ids[:, :, None] == names[None, None, :], axis=1)
    before = (jnp.arange(tokens)[:, None] > jnp.arange(tokens)[None, :]).astype(jnp.bfloat16)
    rank = jnp.dot(before, named.astype(jnp.bfloat16), preferred_element_type=jnp.float32)
    rank = jnp.where(named, rank.astype(jnp.int32), capacity).T
    rank = rank.reshape(16, 2, 2, 2, tokens).transpose(1, 3, 0, 2, 4).reshape(4, 32, tokens)
    slot = jnp.arange(capacity, dtype=jnp.int32)
    chosen = rank[:, :, None, :] == slot[None, None, :, None]
    return chosen.astype(jnp.bfloat16).reshape(4, 32 * capacity, tokens)


def silu(v):
    return v / (1.0 + jnp.exp(-v))


def expert_kernel(
    tok, plc, w, out,
    tok_all, plc_all, outgoing, rows, keep, other, local, hidden, hidden_t, column, upper, lower, inverse, block, block_u,
    give, take, final, relay,
    near_s, near_r, leg_s, leg_r, far_s, far_r, w_s, w_r, r_s, r_r, own,
):
    z, y, c = lax.axis_index("z"), lax.axis_index("y"), lax.axis_index("core")
    xh, xl = lax.axis_index("xh"), lax.axis_index("xl")
    me_x = xh * 2 + xl
    me_p = (z * 4 + y) * 2 + c
    partner = (z, y, xh, c, 1 - xl)

    def on_ring(r):
        p = (me_x + r) % 4
        return p, (z, y, p // 2, c, p % 2)

    def on_plane(k):
        p = (me_p + k) % 32
        return p, (p // 8, (p // 2) % 4, xh, p % 2, xl)

    def remote(src, dst, send, recv, device):
        return pltpu.make_async_remote_copy(src, dst, send, recv, device_id=device, device_id_type=MESH)

    keeping = pltpu.make_async_copy(w.at[xl], keep, own.at[0])
    keeping.start()
    here = [
        pltpu.make_async_copy(tok, tok_all.at[me_x], own.at[1]),
        pltpu.make_async_copy(plc.at[me_x], plc_all.at[me_x], own.at[2]),
    ]
    for copy in here:
        copy.start()

    barrier = pltpu.get_barrier_semaphore()
    for r in range(1, 4):
        pl.semaphore_signal(barrier, 1, device_id=on_ring(r)[1], device_id_type=MESH)

    def greet(k, carry):
        pl.semaphore_signal(barrier, 1, device_id=on_plane(k)[1], device_id_type=MESH)
        return carry

    lax.fori_loop(1, 32, greet, 0)
    pl.semaphore_wait(barrier, 34)

    right, to_right = on_ring(1)
    opposite, to_opposite = on_ring(2)
    left, to_left = on_ring(3)
    first, second = pl.ds(0, 32), pl.ds(32, 32)
    tok_right = remote(tok, tok_all.at[me_x], near_s.at[0], near_r.at[0], to_right)
    tok_left = remote(tok, tok_all.at[me_x], near_s.at[1], near_r.at[1], to_left)
    on_right = remote(tok_all.at[left, first], tok_all.at[left, first], near_s.at[2], near_r.at[2], to_right)
    on_left = remote(tok_all.at[right, second], tok_all.at[right, second], near_s.at[3], near_r.at[3], to_left)
    named = [
        remote(plc.at[p], plc_all.at[me_x], near_s.at[i], near_r.at[i], device)
        for i, p, device in ((4, right, to_right), (5, opposite, to_opposite), (6, left, to_left))
    ]
    tok_right.start()
    tok_left.start()
    for copy in named:
        copy.start()
    upper[...] = jnp.zeros_like(upper)
    final[...] = jnp.zeros_like(final)
    tok_right.wait_recv()
    on_right.start()
    tok_left.wait_recv()
    on_left.start()
    for copy in here + named:
        copy.wait()
    tok_right.wait_send()
    tok_left.wait_send()
    on_right.wait()
    on_left.wait()

    weights = []
    for i, (at, size) in enumerate(parts):
        columns = pl.ds(at, size)
        weights.append(remote(w.at[1 - xl, :, columns], other.at[:, columns], w_s.at[i], w_r.at[i], partner))
        weights[i].start()

    def select(i, carry):
        columns = pl.ds(pl.multiple_of(i * 512, 512), 512)
        picked = [
            jnp.dot(plc_all[b], tok_all[b, :, columns], preferred_element_type=jnp.float32).reshape(32, 8, 512)
            for b in range(4)
        ]
        outgoing[:, columns] = jnp.stack(picked, axis=1).reshape(1024, 512).astype(jnp.bfloat16)
        return carry

    lax.fori_loop(0, 8, select, 0)

    def plane(dz, dy, dc):
        return (z + dz) % 4, (y + dy) % 4, xh, (c + dc) % 2, xl

    def picked_for(device):
        p = (device[0] * 4 + device[1]) * 2 + device[3]
        return outgoing.at[pl.ds(pl.multiple_of(p * 32, 32), 32), :]

    first_leg, far = [], {}
    for k in range(1, 32):
        dz, dy, dc = k // 8, (k // 2) % 4, k % 2
        dest, slot = plane(dz, dy, dc), rows.at[pl.ds(32 * k, 32), :]
        if (dz == 2 and dc == 0) or (dy == 2 and dc == 1):
            j = len(first_leg)
            via = plane(3, dy, 0) if dc == 0 else plane(dz, 3, 1)
            onward = plane(3, 0, 0) if dc == 0 else plane(0, 3, 0)
            held = relay.at[pl.ds(32 * j, 32), :]
            first_leg.append((k, remote(picked_for(dest), held, leg_s.at[j], leg_r.at[j], via)))
            far[k] = remote(held, slot, far_s.at[k], far_r.at[k], onward)
        else:
            far[k] = remote(picked_for(dest), slot, far_s.at[k], far_r.at[k], dest)
    relayed = [k for k, _ in first_leg]
    for _, copy in first_leg:
        copy.start()
    for k in range(1, 32):
        if k not in relayed:
            far[k].start()
    kept = pltpu.make_async_copy(
        outgoing.at[pl.ds(pl.multiple_of(me_p * 32, 32), 32), :], rows.at[pl.ds(0, 32), :], own.at[1]
    )
    kept.start()
    kept.wait()
    keeping.wait()

    for k, copy in first_leg:
        copy.wait_recv()
        far[k].start()
    for g in (1, 3, 0, 2):
        for k in range(max(1, 8 * g), 8 * g + 8):
            far[k].wait()
        at = pl.ds(256 * g, 256)
        local[at, :] = jnp.dot(rows[at, :], keep[...], preferred_element_type=jnp.float32)
    for _, copy in first_leg:
        copy.wait_send()

    def project(at, size):
        def tile(i, carry):
            some = pl.ds(pl.multiple_of(i * 512, 512), 512)
            theirs = jnp.dot(rows[some, :], other[:, at : at + size], preferred_element_type=jnp.float32)
            mine = local[some, at : at + size]
            gate = jnp.where(xl == 0, mine, theirs)
            up = jnp.where(xl == 0, theirs, mine)
            h = silu(gate) * up
            hidden[some, at : at + size] = h.astype(jnp.bfloat16)
            hidden_t[at : at + size, some] = h.T.astype(jnp.bfloat16)
            return carry

        lax.fori_loop(0, 2, tile, 0)

    eye = (lax.broadcasted_iota(jnp.int32, (B, B), 0) == lax.broadcasted_iota(jnp.int32, (B, B), 1)).astype(jnp.float32)

    def put_u(i, v):
        block_u[8 * i : 8 * i + 8, :] = v

    def factor_column(k):
        o, n = B * k, B * (k + 1)
        column[0:n, :] = jnp.dot(hidden_t[0:n, :], hidden[:, o:n], preferred_element_type=jnp.float32) * (1.0 / rows_mean)
        for i in range(k):
            a, b = B * i, B * (i + 1)
            solved = dot(inverse[i], column[a:b, :])
            upper[a:b, o:n] = solved
            if i + 1 < k:
                column[b:o, :] -= dot(lower[b:o, a:b], solved)
        pivot = column[o:n, :] + damping * damping * eye
        if k:
            turned = upper[0:o, o:n].T
            lower[o:n, 0:o] = turned
            pivot = pivot - dot(turned, upper[0:o, o:n])
        block[...] = pivot

        def put_l(i, v):
            inverse[k, 8 * i : 8 * i + 8, :] = v

        def once(i, carry):
            factor_block(lambda i: block[8 * i : 8 * i + 8, :], put_u, put_l)
            return carry

        lax.fori_loop(0, 1, once, 0)
        upper[o:n, o:n] = block_u[...]

    half = final.shape[0]
    pieces = []
    for k in range(NB):
        for i, (at, size) in enumerate(parts):
            if at == B * k:
                weights[i].wait_recv()
                project(at, size)
        factor_column(k)
        n = min(half, B * (k + 1))
        give[k, 0:n, :] = upper[pl.ds(pl.multiple_of((1 - xl) * half, half), n), B * k : B * k + B].astype(jnp.bfloat16)
        pieces.append(remote(give.at[k, pl.ds(0, n)], take.at[k, pl.ds(0, n)], r_s.at[k], r_r.at[k], partner))
        pieces[k].start()
    mine = pltpu.make_async_copy(upper.at[pl.ds(pl.multiple_of(xl * half, half), half), :], out.at[xl], own.at[0])
    mine.start()
    for k in range(NB):
        n = min(half, B * (k + 1))
        pieces[k].wait()
        final[0:n, B * k : B * k + B] = take[k, 0:n, :].astype(jnp.float32)
    theirs = pltpu.make_async_copy(final, out.at[1 - xl], own.at[1])
    theirs.start()
    for copy in weights:
        copy.wait_send()
    mine.wait()
    theirs.wait()


def on_device(tokens, expert_ids, gate_up):
    depth = tokens.shape[1]
    width = gate_up.shape[2]
    half = width // 2
    placing = slots(expert_ids)
    anywhere = pl.BlockSpec(memory_space=pl.ANY)
    dma = pltpu.SemaphoreType.DMA
    bf16, f32 = jnp.bfloat16, jnp.float32
    return pl.pallas_call(
        expert_kernel,
        out_shape=jax.ShapeDtypeStruct((2, half, width), f32),
        in_specs=[anywhere] * 3,
        out_specs=anywhere,
        scratch_shapes=[
            pltpu.VMEM((4, 64, depth), bf16),
            pltpu.VMEM((4, 256, 64), bf16),
            pltpu.VMEM((1024, depth), bf16),
            pltpu.VMEM((1024, depth), bf16),
            pltpu.VMEM((depth, width), bf16),
            pltpu.VMEM((depth, width), bf16),
            pltpu.VMEM((1024, width), f32),
            pltpu.VMEM((1024, width), bf16),
            pltpu.VMEM((width, 1024), bf16),
            pltpu.VMEM((width, B), f32),
            pltpu.VMEM((width, width), f32),
            pltpu.VMEM((width, width), f32),
            pltpu.VMEM((NB, B, B), f32),
            pltpu.VMEM((B, B), f32),
            pltpu.VMEM((B, B), f32),
            pltpu.VMEM((NB, half, B), bf16),
            pltpu.VMEM((NB, half, B), bf16),
            pltpu.VMEM((half, width), f32),
            pltpu.VMEM((256, depth), bf16),
            dma((7,)),
            dma((7,)),
            dma((8,)),
            dma((8,)),
            dma((32,)),
            dma((32,)),
            dma((len(parts),)),
            dma((len(parts),)),
            dma((NB,)),
            dma((NB,)),
            dma((3,)),
        ],
        compiler_params=pltpu.CompilerParams(collective_id=1, has_side_effects=True, vmem_limit_bytes=60 << 20),
        name="expert_factor",
    )(tokens, placing, gate_up)


def solution(mesh):
    split = Mesh(mesh.devices.reshape(4, 4, 2, 2, 2), ("z", "y", "xh", "core", "xl"))
    every = ("z", "y", "xh", "core", "xl")
    holders = ("z", "y", "xh", "core")
    return jax.shard_map(
        on_device,
        mesh=split,
        in_specs=(P(every, None), P(every, None), P(holders, None, "xl")),
        out_specs=P(holders, "xl", None),
        check_vma=False,
    )
```

```python
import jax
import jax.numpy as jnp
from jax import lax
from jax.sharding import Mesh, PartitionSpec as P
from jax.experimental import pallas as pl
from jax.experimental.pallas import tpu as pltpu

damping = 0.25
capacity = 8
rows_mean = 512
experts = 128
parts = ((0, 256), (256, 256), (512, 128), (640, 128))
MESH = pl.DeviceIdType.MESH

N=768; B=128; NB=N//B
HI=lax.Precision.HIGHEST
def dotT(a,b):
    return lax.dot_general(a,b,(((0,),(0,)),((),())),precision=HI,preferred_element_type=jnp.float32)
def dot(a,b):
    return lax.dot_general(a,b,(((1,),(0,)),((),())),precision=HI,preferred_element_type=jnp.float32)
def rep(v,s):
    return jnp.take_along_axis(v, jnp.full((8,128),s,jnp.int32), axis=0)
def factor_block(get, put_u, put_l):
    sub=lax.broadcasted_iota(jnp.int32,(8,128),0); lane=lax.broadcasted_iota(jnp.int32,(8,128),1)
    A=[get(i) for i in range(16)]
    E=[jnp.where(lane==sub+8*i,1.0,0.0).astype(jnp.float32) for i in range(16)]
    for q in range(16):
        C=[[jnp.broadcast_to(A[i][:,8*q+m:8*q+m+1],(8,128)) for m in range(8)] for i in range(q,16)]
        p={(j,m):rep(C[0][m],j) for j in range(8) for m in range(j,8)}
        t=[rep(A[q],j) for j in range(8)]
        e=[rep(E[q],j) for j in range(8)]
        pivot=jnp.zeros((8,128),jnp.float32)
        for j in range(8):
            inv=1.0/p[j,j]
            pivot=jnp.where(sub==j,p[j,j],pivot)
            f={m:p[j,m]*inv for m in range(j+1,8)}
            for k in range(j+1,8):
                for m in range(k,8):
                    p[k,m]=p[k,m]-p[j,k]*f[m]
            for m in range(j+1,8):
                t[m]=t[m]-f[m]*t[j]
                e[m]=e[m]-f[m]*e[j]
            ts=t[j]*inv; es=e[j]*inv
            for i in range(q+1,16):
                c=C[i-q]
                for m in range(j+1,8):
                    c[m]=c[m]-c[j]*f[m]
                A[i]=A[i]-c[j]*ts
                E[i]=E[i]-c[j]*es
        rs=lax.rsqrt(pivot)
        u=t[0]; l=e[0]
        for j in range(1,8):
            u=jnp.where(sub==j,t[j],u); l=jnp.where(sub==j,e[j],l)
        put_u(q, jnp.where(lane>=sub+8*q,u*rs,0.0)); put_l(q, l*rs)


def slots(ids):
    tokens = ids.shape[0]
    names = jnp.arange(experts, dtype=jnp.int32)
    named = jnp.any(ids[:, :, None] == names[None, None, :], axis=1)
    before = (jnp.arange(tokens)[:, None] > jnp.arange(tokens)[None, :]).astype(jnp.bfloat16)
    rank = jnp.dot(before, named.astype(jnp.bfloat16), preferred_element_type=jnp.float32)
    rank = jnp.where(named, rank.astype(jnp.int32), capacity).T
    rank = rank.reshape(16, 2, 2, 2, tokens).transpose(1, 3, 0, 2, 4).reshape(4, 32, tokens)
    slot = jnp.arange(capacity, dtype=jnp.int32)
    chosen = rank[:, :, None, :] == slot[None, None, :, None]
    return chosen.astype(jnp.bfloat16).reshape(4, 32 * capacity, tokens)


def silu(v):
    return v / (1.0 + jnp.exp(-v))


def expert_kernel(
    tok, plc, w, out,
    tok_all, plc_all, outgoing, rows, keep, other, local, hidden, hidden_t, column, upper, lower, inverse, block, block_u,
    give, take, final, relay,
    near_s, near_r, leg_s, leg_r, far_s, far_r, w_s, w_r, r_s, r_r, own,
):
    z, y, c = lax.axis_index("z"), lax.axis_index("y"), lax.axis_index("core")
    xh, xl = lax.axis_index("xh"), lax.axis_index("xl")
    me_x = xh * 2 + xl
    me_p = (z * 4 + y) * 2 + c
    partner = (z, y, xh, c, 1 - xl)

    def on_ring(r):
        p = (me_x + r) % 4
        return p, (z, y, p // 2, c, p % 2)

    def on_plane(k):
        p = (me_p + k) % 32
        return p, (p // 8, (p // 2) % 4, xh, p % 2, xl)

    def remote(src, dst, send, recv, device):
        return pltpu.make_async_remote_copy(src, dst, send, recv, device_id=device, device_id_type=MESH)

    keeping = pltpu.make_async_copy(w.at[xl], keep, own.at[0])
    keeping.start()
    here = [
        pltpu.make_async_copy(tok, tok_all.at[me_x], own.at[1]),
        pltpu.make_async_copy(plc.at[me_x], plc_all.at[me_x], own.at[2]),
    ]
    for copy in here:
        copy.start()

    barrier = pltpu.get_barrier_semaphore()
    for r in range(1, 4):
        pl.semaphore_signal(barrier, 1, device_id=on_ring(r)[1], device_id_type=MESH)

    def greet(k, carry):
        pl.semaphore_signal(barrier, 1, device_id=on_plane(k)[1], device_id_type=MESH)
        return carry

    lax.fori_loop(1, 32, greet, 0)
    pl.semaphore_wait(barrier, 34)

    right, to_right = on_ring(1)
    opposite, to_opposite = on_ring(2)
    left, to_left = on_ring(3)
    first, second = pl.ds(0, 32), pl.ds(32, 32)
    tok_right = remote(tok, tok_all.at[me_x], near_s.at[0], near_r.at[0], to_right)
    tok_left = remote(tok, tok_all.at[me_x], near_s.at[1], near_r.at[1], to_left)
    on_right = remote(tok_all.at[left, first], tok_all.at[left, first], near_s.at[2], near_r.at[2], to_right)
    on_left = remote(tok_all.at[right, second], tok_all.at[right, second], near_s.at[3], near_r.at[3], to_left)
    named = [
        remote(plc.at[p], plc_all.at[me_x], near_s.at[i], near_r.at[i], device)
        for i, p, device in ((4, right, to_right), (5, opposite, to_opposite), (6, left, to_left))
    ]
    tok_right.start()
    tok_left.start()
    for copy in named:
        copy.start()
    upper[...] = jnp.zeros_like(upper)
    final[...] = jnp.zeros_like(final)
    tok_right.wait_recv()
    on_right.start()
    tok_left.wait_recv()
    on_left.start()
    for copy in here + named:
        copy.wait()
    tok_right.wait_send()
    tok_left.wait_send()
    on_right.wait()
    on_left.wait()

    weights = []
    for i, (at, size) in enumerate(parts):
        columns = pl.ds(at, size)
        weights.append(remote(w.at[1 - xl, :, columns], other.at[:, columns], w_s.at[i], w_r.at[i], partner))
        weights[i].start()

    def select(i, carry):
        columns = pl.ds(pl.multiple_of(i * 512, 512), 512)
        picked = [
            jnp.dot(plc_all[b], tok_all[b, :, columns], preferred_element_type=jnp.float32).reshape(32, 8, 512)
            for b in range(4)
        ]
        outgoing[:, columns] = jnp.stack(picked, axis=1).reshape(1024, 512).astype(jnp.bfloat16)
        return carry

    lax.fori_loop(0, 8, select, 0)

    def plane(dz, dy, dc):
        return (z + dz) % 4, (y + dy) % 4, xh, (c + dc) % 2, xl

    def picked_for(device):
        p = (device[0] * 4 + device[1]) * 2 + device[3]
        return outgoing.at[pl.ds(pl.multiple_of(p * 32, 32), 32), :]

    first_leg, far = [], {}
    for k in range(1, 32):
        dz, dy, dc = k // 8, (k // 2) % 4, k % 2
        dest, slot = plane(dz, dy, dc), rows.at[pl.ds(32 * k, 32), :]
        if (dz == 2 and dc == 0) or (dy == 2 and dc == 1):
            j = len(first_leg)
            via = plane(3, dy, 0) if dc == 0 else plane(dz, 3, 1)
            onward = plane(3, 0, 0) if dc == 0 else plane(0, 3, 0)
            held = relay.at[pl.ds(32 * j, 32), :]
            first_leg.append((k, remote(picked_for(dest), held, leg_s.at[j], leg_r.at[j], via)))
            far[k] = remote(held, slot, far_s.at[k], far_r.at[k], onward)
        else:
            far[k] = remote(picked_for(dest), slot, far_s.at[k], far_r.at[k], dest)
    relayed = [k for k, _ in first_leg]
    for _, copy in first_leg:
        copy.start()
    for k in range(1, 32):
        if k not in relayed:
            far[k].start()
    kept = pltpu.make_async_copy(
        outgoing.at[pl.ds(pl.multiple_of(me_p * 32, 32), 32), :], rows.at[pl.ds(0, 32), :], own.at[1]
    )
    kept.start()
    kept.wait()
    keeping.wait()

    for k, copy in first_leg:
        copy.wait_recv()
        far[k].start()
    for g in (1, 3, 0, 2):
        for k in range(max(1, 8 * g), 8 * g + 8):
            far[k].wait()
        at = pl.ds(256 * g, 256)
        local[at, :] = jnp.dot(rows[at, :], keep[...], preferred_element_type=jnp.float32)
    for _, copy in first_leg:
        copy.wait_send()

    def project(at, size):
        def tile(i, carry):
            some = pl.ds(pl.multiple_of(i * 512, 512), 512)
            theirs = jnp.dot(rows[some, :], other[:, at : at + size], preferred_element_type=jnp.float32)
            mine = local[some, at : at + size]
            gate = jnp.where(xl == 0, mine, theirs)
            up = jnp.where(xl == 0, theirs, mine)
            h = silu(gate) * up
            hidden[some, at : at + size] = h.astype(jnp.bfloat16)
            hidden_t[at : at + size, some] = h.T.astype(jnp.bfloat16)
            return carry

        lax.fori_loop(0, 2, tile, 0)

    eye = (lax.broadcasted_iota(jnp.int32, (B, B), 0) == lax.broadcasted_iota(jnp.int32, (B, B), 1)).astype(jnp.float32)

    def put_u(i, v):
        block_u[8 * i : 8 * i + 8, :] = v

    def factor_column(k):
        o, n = B * k, B * (k + 1)
        column[0:n, :] = jnp.dot(hidden_t[0:n, :], hidden[:, o:n], preferred_element_type=jnp.float32) * (1.0 / rows_mean)
        for i in range(k):
            a, b = B * i, B * (i + 1)
            solved = dot(inverse[i], column[a:b, :])
            upper[a:b, o:n] = solved
            if i + 1 < k:
                column[b:o, :] -= dot(lower[b:o, a:b], solved)
        pivot = column[o:n, :] + damping * damping * eye
        if k:
            turned = upper[0:o, o:n].T
            lower[o:n, 0:o] = turned
            pivot = pivot - dot(turned, upper[0:o, o:n])
        block[...] = pivot

        def put_l(i, v):
            inverse[k, 8 * i : 8 * i + 8, :] = v

        def once(i, carry):
            factor_block(lambda i: block[8 * i : 8 * i + 8, :], put_u, put_l)
            return carry

        lax.fori_loop(0, 1, once, 0)
        upper[o:n, o:n] = block_u[...]

    half = final.shape[0]
    pieces = []
    for k in range(NB):
        for i, (at, size) in enumerate(parts):
            if at == B * k:
                weights[i].wait_recv()
                project(at, size)
        factor_column(k)
        n = min(half, B * (k + 1))
        give[k, 0:n, :] = upper[pl.ds(pl.multiple_of((1 - xl) * half, half), n), B * k : B * k + B].astype(jnp.bfloat16)
        pieces.append(remote(give.at[k, pl.ds(0, n)], take.at[k, pl.ds(0, n)], r_s.at[k], r_r.at[k], partner))
        pieces[k].start()
    mine = pltpu.make_async_copy(upper.at[pl.ds(pl.multiple_of(xl * half, half), half), :], out.at[xl], own.at[0])
    mine.start()
    for k in range(NB):
        n = min(half, B * (k + 1))
        pieces[k].wait()
        final[0:n, B * k : B * k + B] = take[k, 0:n, :].astype(jnp.float32)
    theirs = pltpu.make_async_copy(final, out.at[1 - xl], own.at[1])
    theirs.start()
    for copy in weights:
        copy.wait_send()
    mine.wait()
    theirs.wait()


def on_device(tokens, expert_ids, gate_up):
    depth = tokens.shape[1]
    width = gate_up.shape[2]
    half = width // 2
    placing = slots(expert_ids)
    anywhere = pl.BlockSpec(memory_space=pl.ANY)
    dma = pltpu.SemaphoreType.DMA
    bf16, f32 = jnp.bfloat16, jnp.float32
    return pl.pallas_call(
        expert_kernel,
        out_shape=jax.ShapeDtypeStruct((2, half, width), f32),
        in_specs=[anywhere] * 3,
        out_specs=anywhere,
        scratch_shapes=[
            pltpu.VMEM((4, 64, depth), bf16),
            pltpu.VMEM((4, 256, 64), bf16),
            pltpu.VMEM((1024, depth), bf16),
            pltpu.VMEM((1024, depth), bf16),
            pltpu.VMEM((depth, width), bf16),
            pltpu.VMEM((depth, width), bf16),
            pltpu.VMEM((1024, width), f32),
            pltpu.VMEM((1024, width), bf16),
            pltpu.VMEM((width, 1024), bf16),
            pltpu.VMEM((width, B), f32),
            pltpu.VMEM((width, width), f32),
            pltpu.VMEM((width, width), f32),
            pltpu.VMEM((NB, B, B), f32),
            pltpu.VMEM((B, B), f32),
            pltpu.VMEM((B, B), f32),
            pltpu.VMEM((NB, half, B), bf16),
            pltpu.VMEM((NB, half, B), bf16),
            pltpu.VMEM((half, width), f32),
            pltpu.VMEM((256, depth), bf16),
            dma((7,)),
            dma((7,)),
            dma((8,)),
            dma((8,)),
            dma((32,)),
            dma((32,)),
            dma((len(parts),)),
            dma((len(parts),)),
            dma((NB,)),
            dma((NB,)),
            dma((3,)),
        ],
        compiler_params=pltpu.CompilerParams(collective_id=1, has_side_effects=True, vmem_limit_bytes=60 << 20),
        name="expert_factor",
    )(tokens, placing, gate_up)


def solution(mesh):
    split = Mesh(mesh.devices.reshape(4, 4, 2, 2, 2), ("z", "y", "xh", "core", "xl"))
    every = ("z", "y", "xh", "core", "xl")
    holders = ("z", "y", "xh", "core")
    return jax.shard_map(
        on_device,
        mesh=split,
        in_specs=(P(every, None), P(every, None), P(holders, None, "xl")),
        out_specs=P(holders, "xl", None),
        check_vma=False,
    )
```

```python
import jax
import jax.numpy as jnp
from jax import lax
from jax.sharding import Mesh, PartitionSpec as P
from jax.experimental import pallas as pl
from jax.experimental.pallas import tpu as pltpu

damping = 0.25
capacity = 8
rows_mean = 512
experts = 128
parts = ((0, 256), (256, 256), (512, 128), (640, 128))
MESH = pl.DeviceIdType.MESH

N=768; B=128; NB=N//B
HI=lax.Precision.HIGHEST
def dotT(a,b):
    return lax.dot_general(a,b,(((0,),(0,)),((),())),precision=HI,preferred_element_type=jnp.float32)
def dot(a,b):
    return lax.dot_general(a,b,(((1,),(0,)),((),())),precision=HI,preferred_element_type=jnp.float32)
def rep(v,s):
    return jnp.take_along_axis(v, jnp.full((8,128),s,jnp.int32), axis=0)
def factor_block(get, put_u, put_l):
    sub=lax.broadcasted_iota(jnp.int32,(8,128),0); lane=lax.broadcasted_iota(jnp.int32,(8,128),1)
    A=[get(i) for i in range(16)]
    E=[jnp.where(lane==sub+8*i,1.0,0.0).astype(jnp.float32) for i in range(16)]
    for q in range(16):
        C=[[jnp.broadcast_to(A[i][:,8*q+m:8*q+m+1],(8,128)) for m in range(8)] for i in range(q,16)]
        p={(j,m):rep(C[0][m],j) for j in range(8) for m in range(j,8)}
        t=[rep(A[q],j) for j in range(8)]
        e=[rep(E[q],j) for j in range(8)]
        pivot=jnp.zeros((8,128),jnp.float32)
        for j in range(8):
            inv=1.0/p[j,j]
            pivot=jnp.where(sub==j,p[j,j],pivot)
            f={m:p[j,m]*inv for m in range(j+1,8)}
            for k in range(j+1,8):
                for m in range(k,8):
                    p[k,m]=p[k,m]-p[j,k]*f[m]
            for m in range(j+1,8):
                t[m]=t[m]-f[m]*t[j]
                e[m]=e[m]-f[m]*e[j]
            ts=t[j]*inv; es=e[j]*inv
            for i in range(q+1,16):
                c=C[i-q]
                for m in range(j+1,8):
                    c[m]=c[m]-c[j]*f[m]
                A[i]=A[i]-c[j]*ts
                E[i]=E[i]-c[j]*es
        rs=lax.rsqrt(pivot)
        u=t[0]; l=e[0]
        for j in range(1,8):
            u=jnp.where(sub==j,t[j],u); l=jnp.where(sub==j,e[j],l)
        put_u(q, jnp.where(lane>=sub+8*q,u*rs,0.0)); put_l(q, l*rs)


def slots(ids):
    tokens = ids.shape[0]
    names = jnp.arange(experts, dtype=jnp.int32)
    named = jnp.any(ids[:, :, None] == names[None, None, :], axis=1)
    before = (jnp.arange(tokens)[:, None] > jnp.arange(tokens)[None, :]).astype(jnp.bfloat16)
    rank = jnp.dot(before, named.astype(jnp.bfloat16), preferred_element_type=jnp.float32)
    rank = jnp.where(named, rank.astype(jnp.int32), capacity).T
    rank = rank.reshape(16, 2, 2, 2, tokens).transpose(1, 3, 0, 2, 4).reshape(4, 32, tokens)
    slot = jnp.arange(capacity, dtype=jnp.int32)
    chosen = rank[:, :, None, :] == slot[None, None, :, None]
    return chosen.astype(jnp.bfloat16).reshape(4, 32 * capacity, tokens)


def silu(v):
    return v / (1.0 + jnp.exp(-v))


def expert_kernel(
    tok, plc, w, out,
    tok_all, plc_all, outgoing, rows, keep, other, local, hidden, hidden_t, column, upper, lower, inverse, block, block_u,
    give, take, final, relay,
    near_s, near_r, leg_s, leg_r, far_s, far_r, w_s, w_r, r_s, r_r, own,
):
    z, y, c = lax.axis_index("z"), lax.axis_index("y"), lax.axis_index("core")
    xh, xl = lax.axis_index("xh"), lax.axis_index("xl")
    me_x = xh * 2 + xl
    me_p = (z * 4 + y) * 2 + c
    partner = (z, y, xh, c, 1 - xl)

    def on_ring(r):
        p = (me_x + r) % 4
        return p, (z, y, p // 2, c, p % 2)

    def on_plane(k):
        p = (me_p + k) % 32
        return p, (p // 8, (p // 2) % 4, xh, p % 2, xl)

    def remote(src, dst, send, recv, device):
        return pltpu.make_async_remote_copy(src, dst, send, recv, device_id=device, device_id_type=MESH)

    keeping = pltpu.make_async_copy(w.at[xl], keep, own.at[0])
    keeping.start()
    here = [
        pltpu.make_async_copy(tok, tok_all.at[me_x], own.at[1]),
        pltpu.make_async_copy(plc.at[me_x], plc_all.at[me_x], own.at[2]),
    ]
    for copy in here:
        copy.start()

    barrier = pltpu.get_barrier_semaphore()
    for r in range(1, 4):
        pl.semaphore_signal(barrier, 1, device_id=on_ring(r)[1], device_id_type=MESH)

    def greet(k, carry):
        pl.semaphore_signal(barrier, 1, device_id=on_plane(k)[1], device_id_type=MESH)
        return carry

    lax.fori_loop(1, 32, greet, 0)
    pl.semaphore_wait(barrier, 34)

    right, to_right = on_ring(1)
    opposite, to_opposite = on_ring(2)
    left, to_left = on_ring(3)
    first, second = pl.ds(0, 32), pl.ds(32, 32)
    tok_right = remote(tok, tok_all.at[me_x], near_s.at[0], near_r.at[0], to_right)
    tok_left = remote(tok, tok_all.at[me_x], near_s.at[1], near_r.at[1], to_left)
    on_right = remote(tok_all.at[left, first], tok_all.at[left, first], near_s.at[2], near_r.at[2], to_right)
    on_left = remote(tok_all.at[right, second], tok_all.at[right, second], near_s.at[3], near_r.at[3], to_left)
    named = [
        remote(plc.at[p], plc_all.at[me_x], near_s.at[i], near_r.at[i], device)
        for i, p, device in ((4, right, to_right), (5, opposite, to_opposite), (6, left, to_left))
    ]
    tok_right.start()
    tok_left.start()
    for copy in named:
        copy.start()
    upper[...] = jnp.zeros_like(upper)
    final[...] = jnp.zeros_like(final)
    tok_right.wait_recv()
    on_right.start()
    tok_left.wait_recv()
    on_left.start()
    for copy in here + named:
        copy.wait()
    tok_right.wait_send()
    tok_left.wait_send()
    on_right.wait()
    on_left.wait()

    weights = []
    for i, (at, size) in enumerate(parts):
        columns = pl.ds(at, size)
        weights.append(remote(w.at[1 - xl, :, columns], other.at[:, columns], w_s.at[i], w_r.at[i], partner))
        weights[i].start()

    def select(i, carry):
        columns = pl.ds(pl.multiple_of(i * 512, 512), 512)
        picked = [
            jnp.dot(plc_all[b], tok_all[b, :, columns], preferred_element_type=jnp.float32).reshape(32, 8, 512)
            for b in range(4)
        ]
        outgoing[:, columns] = jnp.stack(picked, axis=1).reshape(1024, 512).astype(jnp.bfloat16)
        return carry

    lax.fori_loop(0, 8, select, 0)

    def plane(dz, dy, dc):
        return (z + dz) % 4, (y + dy) % 4, xh, (c + dc) % 2, xl

    def picked_for(device):
        p = (device[0] * 4 + device[1]) * 2 + device[3]
        return outgoing.at[pl.ds(pl.multiple_of(p * 32, 32), 32), :]

    first_leg, far = [], {}
    for k in range(1, 32):
        dz, dy, dc = k // 8, (k // 2) % 4, k % 2
        dest, slot = plane(dz, dy, dc), rows.at[pl.ds(32 * k, 32), :]
        if (dz == 2 and dc == 0) or (dy == 2 and dc == 1):
            j = len(first_leg)
            via = plane(3, dy, 0) if dc == 0 else plane(dz, 3, 1)
            onward = plane(3, 0, 0) if dc == 0 else plane(0, 3, 0)
            held = relay.at[pl.ds(32 * j, 32), :]
            first_leg.append((k, remote(picked_for(dest), held, leg_s.at[j], leg_r.at[j], via)))
            far[k] = remote(held, slot, far_s.at[k], far_r.at[k], onward)
        else:
            far[k] = remote(picked_for(dest), slot, far_s.at[k], far_r.at[k], dest)
    relayed = [k for k, _ in first_leg]
    for _, copy in first_leg:
        copy.start()
    for k in range(1, 32):
        if k not in relayed:
            far[k].start()
    kept = pltpu.make_async_copy(
        outgoing.at[pl.ds(pl.multiple_of(me_p * 32, 32), 32), :], rows.at[pl.ds(0, 32), :], own.at[1]
    )
    kept.start()
    kept.wait()
    keeping.wait()

    for k, copy in first_leg:
        copy.wait_recv()
        far[k].start()
    for g in (1, 3, 0, 2):
        for k in range(max(1, 8 * g), 8 * g + 8):
            far[k].wait()
        at = pl.ds(256 * g, 256)
        local[at, :] = jnp.dot(rows[at, :], keep[...], preferred_element_type=jnp.float32)
    for _, copy in first_leg:
        copy.wait_send()

    def project(at, size):
        def tile(i, carry):
            some = pl.ds(pl.multiple_of(i * 512, 512), 512)
            theirs = jnp.dot(rows[some, :], other[:, at : at + size], preferred_element_type=jnp.float32)
            mine = local[some, at : at + size]
            gate = jnp.where(xl == 0, mine, theirs)
            up = jnp.where(xl == 0, theirs, mine)
            h = silu(gate) * up
            hidden[some, at : at + size] = h.astype(jnp.bfloat16)
            hidden_t[at : at + size, some] = h.T.astype(jnp.bfloat16)
            return carry

        lax.fori_loop(0, 2, tile, 0)

    eye = (lax.broadcasted_iota(jnp.int32, (B, B), 0) == lax.broadcasted_iota(jnp.int32, (B, B), 1)).astype(jnp.float32)

    def put_u(i, v):
        block_u[8 * i : 8 * i + 8, :] = v

    def factor_column(k):
        o, n = B * k, B * (k + 1)
        column[0:n, :] = jnp.dot(hidden_t[0:n, :], hidden[:, o:n], preferred_element_type=jnp.float32) * (1.0 / rows_mean)
        for i in range(k):
            a, b = B * i, B * (i + 1)
            solved = dot(inverse[i], column[a:b, :])
            upper[a:b, o:n] = solved
            if i + 1 < k:
                column[b:o, :] -= dot(lower[b:o, a:b], solved)
        pivot = column[o:n, :] + damping * damping * eye
        if k:
            turned = upper[0:o, o:n].T
            lower[o:n, 0:o] = turned
            pivot = pivot - dot(turned, upper[0:o, o:n])
        block[...] = pivot

        def put_l(i, v):
            inverse[k, 8 * i : 8 * i + 8, :] = v

        def once(i, carry):
            factor_block(lambda i: block[8 * i : 8 * i + 8, :], put_u, put_l)
            return carry

        lax.fori_loop(0, 1, once, 0)
        upper[o:n, o:n] = block_u[...]

    half = final.shape[0]
    pieces = []

    def receive(k):
        n = min(half, B * (k + 1))
        pieces[k].wait()
        final[0:n, B * k : B * k + B] = take[k, 0:n, :].astype(jnp.float32)

    for k in range(NB):
        if k == NB - 1:
            for i in range(NB - 2):
                receive(i)
        for i, (at, size) in enumerate(parts):
            if at == B * k:
                weights[i].wait_recv()
                project(at, size)
        factor_column(k)
        n = min(half, B * (k + 1))
        give[k, 0:n, :] = upper[pl.ds(pl.multiple_of((1 - xl) * half, half), n), B * k : B * k + B].astype(jnp.bfloat16)
        pieces.append(remote(give.at[k, pl.ds(0, n)], take.at[k, pl.ds(0, n)], r_s.at[k], r_r.at[k], partner))
        pieces[k].start()
    mine = pltpu.make_async_copy(upper.at[pl.ds(pl.multiple_of(xl * half, half), half), :], out.at[xl], own.at[0])
    mine.start()
    for k in range(NB - 2, NB):
        receive(k)
    theirs = pltpu.make_async_copy(final, out.at[1 - xl], own.at[1])
    theirs.start()
    for copy in weights:
        copy.wait_send()
    mine.wait()
    theirs.wait()


def on_device(tokens, expert_ids, gate_up):
    depth = tokens.shape[1]
    width = gate_up.shape[2]
    half = width // 2
    placing = slots(expert_ids)
    anywhere = pl.BlockSpec(memory_space=pl.ANY)
    dma = pltpu.SemaphoreType.DMA
    bf16, f32 = jnp.bfloat16, jnp.float32
    return pl.pallas_call(
        expert_kernel,
        out_shape=jax.ShapeDtypeStruct((2, half, width), f32),
        in_specs=[anywhere] * 3,
        out_specs=anywhere,
        scratch_shapes=[
            pltpu.VMEM((4, 64, depth), bf16),
            pltpu.VMEM((4, 256, 64), bf16),
            pltpu.VMEM((1024, depth), bf16),
            pltpu.VMEM((1024, depth), bf16),
            pltpu.VMEM((depth, width), bf16),
            pltpu.VMEM((depth, width), bf16),
            pltpu.VMEM((1024, width), f32),
            pltpu.VMEM((1024, width), bf16),
            pltpu.VMEM((width, 1024), bf16),
            pltpu.VMEM((width, B), f32),
            pltpu.VMEM((width, width), f32),
            pltpu.VMEM((width, width), f32),
            pltpu.VMEM((NB, B, B), f32),
            pltpu.VMEM((B, B), f32),
            pltpu.VMEM((B, B), f32),
            pltpu.VMEM((NB, half, B), bf16),
            pltpu.VMEM((NB, half, B), bf16),
            pltpu.VMEM((half, width), f32),
            pltpu.VMEM((256, depth), bf16),
            dma((7,)),
            dma((7,)),
            dma((8,)),
            dma((8,)),
            dma((32,)),
            dma((32,)),
            dma((len(parts),)),
            dma((len(parts),)),
            dma((NB,)),
            dma((NB,)),
            dma((3,)),
        ],
        compiler_params=pltpu.CompilerParams(collective_id=1, has_side_effects=True, vmem_limit_bytes=60 << 20),
        name="expert_factor",
    )(tokens, placing, gate_up)


def solution(mesh):
    split = Mesh(mesh.devices.reshape(4, 4, 2, 2, 2), ("z", "y", "xh", "core", "xl"))
    every = ("z", "y", "xh", "core", "xl")
    holders = ("z", "y", "xh", "core")
    return jax.shard_map(
        on_device,
        mesh=split,
        in_specs=(P(every, None), P(every, None), P(holders, None, "xl")),
        out_specs=P(holders, "xl", None),
        check_vma=False,
    )
```
